32 devices in a mesh: dp: 4 (over z), row: 4 (over y, core), col: 2 (over x).
Axes of the slice: x: 2, y: 2, z: 4, core: 2. Of those that a mesh axis runs over, the one named last changes fastest.
Arguments:
- layer_in: bfloat16 [4096, 2048], P(('dp', 'row'), 'col'), may hold values from -6 to 6
- query_weight: bfloat16 [2048, 2048], P('col', 'row'), may hold values from -0.125 to 0.125
- key_weight: bfloat16 [2048, 2048], P('col', 'row'), may hold values from -0.125 to 0.125
- value_weight: bfloat16 [2048, 2048], P('col', 'row'), may hold values from -0.125 to 0.125
- output_weight: bfloat16 [2048, 2048], P('row', 'col'), may hold values from -0.125 to 0.125
- gate_weight: bfloat16 [2048, 8192], P('col', 'row'), may hold values from -0.125 to 0.125
- up_weight: bfloat16 [2048, 8192], P('col', 'row'), may hold values from -0.125 to 0.125
- down_weight: bfloat16 [8192, 2048], P('row', 'col'), may hold values from -0.0625 to 0.0625
- query_gain: float32 [2048], P(('row', 'col')), may hold values from 0.3 to 2.56, as said below
- key_gain: float32 [2048], P(('row', 'col')), may hold values from 0.3 to 2.56, as said below
- mixing_gain: float32 [2048], P('col'), may hold values from 0.5 to 2
- hidden_gain: float32 [2048], P('col'), may hold values from 0.5 to 2
- out_grad: bfloat16 [4096, 2048], P(('dp', 'row'), 'col'), may hold values from -6 to 6
Outputs:
- layer_out: bfloat16 [4096, 2048], P(('dp', 'row'), 'col')
- in_grad: bfloat16 [4096, 2048], P(('dp', 'row'), 'col')
- query_weight_grad: float32 [2048, 2048], P('col', 'row')
- key_weight_grad: float32 [2048, 2048], P('col', 'row')
- value_weight_grad: float32 [2048, 2048], P('col', 'row')
- output_weight_grad: float32 [2048, 2048], P('row', 'col')
- gate_weight_grad: float32 [2048, 8192], P('col', 'row')
- up_weight_grad: float32 [2048, 8192], P('col', 'row')
- down_weight_grad: float32 [8192, 2048], P('row', 'col')
- query_gain_grad: float32 [2048], P(('row', 'col'))
- key_gain_grad: float32 [2048], P(('row', 'col'))
- mixing_gain_grad: float32 [2048], P('col')
- hidden_gain_grad: float32 [2048], P('col')
The draws below stay inside these ranges and needn't reach their ends.
Inputs may be any that keep to these rules, and one draw needn't show every extreme that they name: `query_gain`: positive gains of the query norm. `key_gain`: positive gains of the key norm.
All inputs are finite; a program needn't handle non-finite values.
Results may differ from the reference program's by a relative error of at most 0.018.
Values may be sent and summed in bfloat16 or wider, within the bound.
No kernel may reach another device: no remote copies, remote signals or barrier semaphores. Data moves between devices by JAX's collectives and lax.ppermute only.
A program may use at most 192 MiB of HBM per device.

```python
import math
import jax
import jax.numpy as jnp
from jax import lax

D = 2048
HEADS = 16
HD = 128
FF = 8192
LEN = 1024
TOKENS = 4096
SEQUENCES = 4


def gain_draw(key, constant_salt):
    head_key = jax.random.fold_in(key, 7)
    channel_key = jax.random.fold_in(key, constant_salt)
    head_scale = jnp.exp(jax.random.uniform(head_key, (HEADS, 1), jnp.float32, jnp.log(0.5), jnp.log(1.6)))
    channel = jnp.exp(jax.random.uniform(channel_key, (HEADS, HD), jnp.float32, jnp.log(0.6), jnp.log(1.6)))
    return (head_scale * channel).reshape(D)


def draw_query_gain(key, part):
    return gain_draw(key, 11)


def draw_key_gain(key, part):
    return gain_draw(key, 23)


def block_scale(own_key, shape, pieces, least, high):
    level = 1.0
    for axis_at, shards_of in pieces:
        steps = jax.random.uniform(jax.random.fold_in(jax.random.fold_in(own_key, 6), axis_at), (shards_of,), jnp.float32, least / len(pieces), high / len(pieces))
        level = level * jnp.repeat(jnp.exp(steps), shape[axis_at] // shards_of).reshape((-1,) + (1,) * (len(shape) - 1 - axis_at))
    return level


def normal_values(rng, dims, deviation, most, shards=(), kind=jnp.bfloat16):
    array = deviation * jax.random.normal(rng, dims, jnp.float32)
    if shards:
        array = array * block_scale(rng, dims, shards, -0.22, 0.18)
    return jnp.clip(array, -most, most).astype(kind)


def setup_inputs(seed: int = 0) -> dict:
    keys = jax.random.split(jax.random.key(seed), 14)
    return {
        "layer_in": normal_values(keys[0], (TOKENS, D), 1.0, 6.0, ((0, 16), (1, 2))),
        "query_weight": normal_values(keys[1], (D, D), D ** -0.5, 0.125, ((0, 2), (1, 4))),
        "key_weight": normal_values(keys[2], (D, D), D ** -0.5, 0.125, ((0, 2), (1, 4))),
        "value_weight": normal_values(keys[3], (D, D), D ** -0.5, 0.125, ((0, 2), (1, 4))),
        "output_weight": normal_values(keys[4], (D, D), D ** -0.5, 0.125, ((0, 4), (1, 2))),
        "gate_weight": normal_values(keys[5], (D, FF), D ** -0.5, 0.125, ((0, 2), (1, 4))),
        "up_weight": normal_values(keys[6], (D, FF), D ** -0.5, 0.125, ((0, 2), (1, 4))),
        "down_weight": normal_values(keys[7], (FF, D), FF ** -0.5, 0.0625, ((0, 4), (1, 2))),
        "query_gain": draw_query_gain(jax.random.fold_in(keys[13], 71), 0),
        "key_gain": draw_key_gain(jax.random.fold_in(keys[13], 71), 0),
        "mixing_gain": jnp.clip(jnp.exp(math.log(2.0) - 1.3862944 * jax.random.uniform(keys[10], (D,), jnp.float32) ** block_scale(keys[10], (D,), ((0, 2),), -0.2, 0.2)), 0.5, 2.0),
        "hidden_gain": jnp.clip(jnp.exp(math.log(2.0) - 1.3862944 * jax.random.uniform(keys[11], (D,), jnp.float32) ** block_scale(keys[11], (D,), ((0, 2),), -0.2, 0.2)), 0.5, 2.0),
        "out_grad": normal_values(keys[12], (TOKENS, D), 1.0, 6.0, ((0, 16), (1, 2))),
    }


epsilon = 1e-06
rope_base = 500000.0
masked_value = -1e+30

@jax.custom_vjp
def low(v):
    return lax.optimization_barrier(v.astype(jnp.bfloat16)).astype(jnp.float32)

@jax.custom_vjp
def low_back(v):
    return v

def low_keep(v):
    return (low(v), None)

def low_pass(kept, grad):
    return (grad,)

def back_keep(v):
    return (v, None)

def back_low(kept, grad):
    return (low(grad),)
low.defvjp(low_keep, low_pass)
low_back.defvjp(back_keep, back_low)

def matmul(left_rows, right_rows):
    return jnp.dot(left_rows, right_rows, precision=lax.Precision.HIGHEST, preferred_element_type=jnp.float32)

def rms_scale(values):
    return lax.rsqrt(lax.optimization_barrier(jnp.mean(values * values, axis=-1, keepdims=True)) + epsilon)

def rotary_tables(row_count):
    positions = (jnp.arange(row_count, dtype=jnp.int32) % LEN).astype(jnp.float32)
    exponent = jnp.arange(HD // 2, dtype=jnp.float32) * (2.0 / HD)
    freq_rows = rope_base ** (-exponent)
    angles = positions[:, None] * freq_rows[None, :]
    angles = jnp.concatenate([angles, angles], axis=1)
    return (jnp.cos(angles), jnp.sin(angles))

def turn_half(values):
    first_half = values[..., :HD // 2]
    second_half = values[..., HD // 2:]
    return jnp.concatenate([-second_half, first_half], axis=-1)

def rotate_rows(row_values, cosine_table, sine_table):
    shaped = row_values.reshape(row_values.shape[0], -1, HD)
    turned = shaped * cosine_table[:, None, :] + turn_half(shaped) * sine_table[:, None, :]
    return turned.reshape(row_values.shape[0], -1)

def attend(operands):
    query_seq, key_seq, value_seq = operands
    raw_scores = jnp.einsum('qhe,khe->hqk', query_seq, key_seq, precision=lax.Precision.HIGHEST) * HD ** (-0.5)
    scores = low_back(raw_scores)
    causal = jnp.arange(LEN, dtype=jnp.int32)[:, None] >= jnp.arange(LEN, dtype=jnp.int32)[None, :]
    scores = jnp.where(causal[None], scores, masked_value)
    soft_weights = low(jax.nn.softmax(scores, axis=-1))
    return jnp.einsum('hqk,khe->qhe', soft_weights, value_seq, precision=lax.Precision.HIGHEST)

def forward(layer_in, query_weight, key_weight, value_weight, output_weight, gate_weight, up_weight, down_weight, query_gain, key_gain, mixing_gain, hidden_gain):
    query_raw = low_back(matmul(layer_in, query_weight))
    key_raw = low_back(matmul(layer_in, key_weight))
    value_raw = low_back(matmul(layer_in, value_weight))
    cosine_table, sine_table = rotary_tables(TOKENS)
    queries = low(rotate_rows(query_raw * rms_scale(query_raw) * query_gain, cosine_table, sine_table))
    key_rows = low(rotate_rows(key_raw * rms_scale(key_raw) * key_gain, cosine_table, sine_table))
    value_rows = low(value_raw)
    shape_four = (SEQUENCES, LEN, HEADS, HD)
    mixed = lax.map(jax.checkpoint(attend), (queries.reshape(shape_four), key_rows.reshape(shape_four), value_rows.reshape(shape_four)))
    mixed = low_back(low(mixed.reshape(TOKENS, D)))
    branch = low_back(matmul(mixed, output_weight))
    hidden_state = layer_in + branch * rms_scale(branch) * mixing_gain
    state_low = low(hidden_state)
    gate_rows = low_back(matmul(state_low, gate_weight))
    up_rows = low_back(matmul(state_low, up_weight))
    activated = low(jax.nn.silu(gate_rows) * up_rows)
    down_rows = low_back(matmul(activated, down_weight))
    return hidden_state + down_rows * rms_scale(down_rows) * hidden_gain

def reference(layer_in, query_weight, key_weight, value_weight, output_weight, gate_weight, up_weight, down_weight, query_gain, key_gain, mixing_gain, hidden_gain, out_grad):
    operands = tuple((operand.astype(jnp.float32) for operand in (layer_in, query_weight, key_weight, value_weight, output_weight, gate_weight, up_weight, down_weight, query_gain, key_gain, mixing_gain, hidden_gain)))
    result, pullback = jax.vjp(forward, *operands)
    gradients = pullback(out_grad.astype(jnp.float32))
    return (result.astype(jnp.bfloat16), gradients[0].astype(jnp.bfloat16), gradients[1], gradients[2], gradients[3], gradients[4], gradients[5], gradients[6], gradients[7], gradients[8], gradients[9], gradients[10], gradients[11])
```

```python
from functools import partial

import jax
import jax.numpy as jnp
from jax import lax
from jax.sharding import PartitionSpec as P

D = 2048
HD = 128
LEN = 1024


epsilon = 1e-06
rope_base = 500000.0
masked_value = -1e30


def low(values):
    return values.astype(jnp.bfloat16)


def wide(values):
    return values.astype(jnp.float32)


def swap(values, axis, mask):
    count = lax.axis_size(axis)
    return lax.ppermute(values, axis, [(i, i ^ mask) for i in range(count)])


def take_rows(values, first, count):
    return lax.dynamic_slice_in_dim(values, first, count, axis=0)


def take_columns(values, first, count):
    return lax.dynamic_slice_in_dim(values, first, count, axis=1)


def row_blocks(shard_rows):
    across = swap(shard_rows, "row", 2)
    return [shard_rows, swap(shard_rows, "row", 1), across, swap(across, "row", 1)]


def in_order(blocks):
    row = lax.axis_index("row")
    rows = blocks[0].shape[0]
    result = jnp.concatenate(blocks, axis=0)
    return jnp.concatenate(
        [take_rows(result, (row ^ k) * rows, rows) for k in range(len(blocks))], axis=0
    )


def rows_reduced(block_of):
    first = block_of(0) + wide(swap(low(block_of(1)), "row", 1))
    other = block_of(2) + wide(swap(low(block_of(3)), "row", 1))
    return first + wide(swap(low(other), "row", 2))


def ordered_block(partials, rows):
    row = lax.axis_index("row")
    return lambda k: take_rows(partials, (row ^ k) * rows, rows)


def both_columns(values):
    col = lax.axis_index("col")
    other = swap(values, "col", 1)
    width = values.shape[1]
    pair = jnp.zeros((values.shape[0], 2 * width), values.dtype)
    pair = lax.dynamic_update_slice_in_dim(pair, values, col * width, axis=1)
    return lax.dynamic_update_slice_in_dim(pair, other, (1 - col) * width, axis=1)


def all_features(shard_rows):
    other = swap(shard_rows, "col", 1)
    own_blocks = row_blocks(shard_rows)
    other_blocks = row_blocks(other)
    return own_blocks, jnp.concatenate(
        [jnp.concatenate(own_blocks, axis=0), jnp.concatenate(other_blocks, axis=0)], axis=1
    )


def features_reduced(partials, rows):
    half = partials.shape[1] // 2
    summed = rows_reduced(lambda k: partials[k * rows : (k + 1) * rows])
    return summed[:, :half] + wide(swap(low(summed[:, half:]), "col", 1))


def pair_total(sums):
    return sums + swap(sums, "col", 1)


def head_totals(sums):
    for axis, mask in (("row", 1), ("row", 2), ("col", 1)):
        sums = sums + swap(sums, axis, mask)
    return sums


def sequences_summed(partials):
    if lax.axis_size("dp") != 4:
        return lax.psum(partials, "dp")
    at = lax.axis_index("dp")
    inner = (at == 1) | (at == 2)
    kind = partials.dtype
    to_inner = lax.ppermute(partials, "dp", [(0, 1), (3, 2)])
    half = (wide(partials) + wide(to_inner)).astype(kind)
    across = lax.ppermute(half, "dp", [(1, 2), (2, 1)])
    total = (wide(half) + wide(across)).astype(kind)
    outward = lax.ppermute(total, "dp", [(1, 0), (2, 3)])
    return jnp.where(inner, total, outward)


def weight_total(partials, pieces, axis):
    parts = jnp.split(low(partials), pieces, axis=axis)
    return jnp.concatenate([wide(sequences_summed(part)) for part in parts], axis=axis)


def project(left_rows, right_rows):
    return jnp.dot(left_rows, right_rows, preferred_element_type=jnp.float32)


def project_back(left_rows, right_rows):
    return lax.dot_general(
        left_rows, right_rows, (((1,), (1,)), ((), ())), preferred_element_type=jnp.float32
    )


def outer_sum(left_rows, right_rows):
    return lax.dot_general(
        left_rows, right_rows, (((0,), (0,)), ((), ())), preferred_element_type=jnp.float32
    )


def rotary_tables(row_count):
    positions = (jnp.arange(row_count, dtype=jnp.int32) % LEN).astype(jnp.float32)
    exponent = jnp.arange(HD // 2, dtype=jnp.float32) * (2.0 / HD)
    freq_rows = rope_base ** (-exponent)
    angles = positions[:, None] * freq_rows[None, :]
    angles = jnp.concatenate([angles, angles], axis=1)
    return (jnp.cos(angles), jnp.sin(angles))


def turn_half(values):
    first_half = values[..., : HD // 2]
    second_half = values[..., HD // 2 :]
    return jnp.concatenate([-second_half, first_half], axis=-1)


def turn_back(values):
    first_half = values[..., : HD // 2]
    second_half = values[..., HD // 2 :]
    return jnp.concatenate([second_half, -first_half], axis=-1)


def rotate_rows(row_values, cosine_table, sine_table):
    shaped = row_values.reshape(row_values.shape[0], -1, HD)
    turned = shaped * cosine_table[:, None, :] + turn_half(shaped) * sine_table[:, None, :]
    return turned.reshape(row_values.shape[0], -1)


def unrotate_rows(row_values, cosine_table, sine_table):
    shaped = row_values.reshape(row_values.shape[0], -1, HD)
    turned = shaped * cosine_table[:, None, :] + turn_back(shaped * sine_table[:, None, :])
    return turned.reshape(row_values.shape[0], -1)


def norm_backward(upstream, raw_rows, row_scale, gain_slice, dot_total):
    scaled = upstream * gain_slice
    return (
        row_scale * scaled
        - raw_rows * (row_scale * row_scale * row_scale) * (dot_total / D)[:, None]
    )


def masked_scores(query_block, key_four, first_row, block_rows):
    raw_scores = jnp.einsum(
        "sqhe,skhe->shqk", query_block, key_four, preferred_element_type=jnp.float32
    ) * HD ** (-0.5)
    query_index = first_row + jnp.arange(block_rows, dtype=jnp.int32)
    causal = query_index[:, None] >= jnp.arange(LEN, dtype=jnp.int32)[None, :]
    return jnp.where(causal, raw_scores, masked_value)


def attention_forward(queries, key_rows, value_rows, block_rows):
    group_rows = queries.shape[0]
    seq_count = group_rows // LEN
    query_four = queries.reshape(seq_count, LEN, -1, HD)
    key_four = key_rows.reshape(seq_count, LEN, -1, HD)
    value_four = value_rows.reshape(seq_count, LEN, -1, HD)
    outputs = []
    log_parts = []
    for block_index in range(LEN // block_rows):
        first_row = block_index * block_rows
        query_block = query_four[:, first_row : first_row + block_rows]
        scores = masked_scores(query_block, key_four, first_row, block_rows)
        row_peak = jnp.max(scores, axis=-1, keepdims=True)
        spread = jnp.exp(scores - row_peak)
        row_total = jnp.sum(spread, axis=-1, keepdims=True)
        soft_weights = (spread / row_total).astype(jnp.bfloat16)
        outputs.append(
            jnp.einsum(
                "shqk,skhe->sqhe", soft_weights, value_four, preferred_element_type=jnp.float32
            )
        )
        log_parts.append((row_peak + jnp.log(row_total))[..., 0])
    mixed = jnp.concatenate(outputs, axis=1).reshape(group_rows, -1).astype(jnp.bfloat16)
    return (mixed, jnp.concatenate(log_parts, axis=2))


def attention_backward(queries, key_rows, value_rows, grad_mixed, log_totals, block_rows):
    group_rows = queries.shape[0]
    seq_count = group_rows // LEN
    query_four = queries.reshape(seq_count, LEN, -1, HD)
    key_four = key_rows.reshape(seq_count, LEN, -1, HD)
    value_four = value_rows.reshape(seq_count, LEN, -1, HD)
    grad_four = grad_mixed.reshape(seq_count, LEN, -1, HD)
    score_scale = HD ** (-0.5)
    grad_keys = jnp.zeros(key_four.shape, jnp.float32)
    grad_values = jnp.zeros(value_four.shape, jnp.float32)
    query_parts = []
    for block_index in range(LEN // block_rows):
        first_row = block_index * block_rows
        query_block = query_four[:, first_row : first_row + block_rows]
        grad_block = grad_four[:, first_row : first_row + block_rows]
        scores = masked_scores(query_block, key_four, first_row, block_rows)
        soft_float = jnp.exp(scores - log_totals[:, :, first_row : first_row + block_rows, None])
        soft_weights = soft_float.astype(jnp.bfloat16)
        grad_values = grad_values + jnp.einsum(
            "shqk,sqhe->skhe", soft_weights, grad_block, preferred_element_type=jnp.float32
        )
        grad_soft = jnp.einsum(
            "sqhe,skhe->shqk", grad_block, value_four, preferred_element_type=jnp.float32
        )
        centre = jnp.sum(soft_float * grad_soft, axis=-1, keepdims=True)
        grad_scores = (soft_float * (grad_soft - centre)).astype(jnp.bfloat16)
        query_parts.append(
            jnp.einsum("shqk,skhe->sqhe", grad_scores, key_four, preferred_element_type=jnp.float32)
            * score_scale
        )
        grad_keys = (
            grad_keys
            + jnp.einsum(
                "shqk,sqhe->skhe", grad_scores, query_block, preferred_element_type=jnp.float32
            )
            * score_scale
        )
    grad_queries = jnp.concatenate(query_parts, axis=1).reshape(group_rows, -1)
    return (grad_queries, grad_keys.reshape(group_rows, -1), grad_values.reshape(group_rows, -1))


def local(
    layer_in,
    query_weight,
    key_weight,
    value_weight,
    output_weight,
    gate_weight,
    up_weight,
    down_weight,
    query_gain,
    key_gain,
    mixing_gain,
    hidden_gain,
    out_grad,
):
    rows = layer_in.shape[0]
    tokens = rows * lax.axis_size("row")
    block_rows = min(512, LEN)
    col = lax.axis_index("col")
    cosine_table, sine_table = rotary_tables(tokens)

    share = query_weight.shape[1] // 2
    hidden = gate_weight.shape[1] // 2
    own_projection = jnp.concatenate(
        [take_columns(w, col * share, share) for w in (query_weight, key_weight, value_weight)], axis=1
    )
    other_projection = jnp.concatenate(
        [take_columns(w, (1 - col) * share, share) for w in (query_weight, key_weight, value_weight)],
        axis=1,
    )

    gathered_in = in_order(row_blocks(layer_in))

    sent = low(project(gathered_in, other_projection))
    kept = project(gathered_in, own_projection)
    got_qk = swap(sent[:, : 2 * share], "col", 1)
    got_v = swap(sent[:, 2 * share :], "col", 1)
    query_raw = kept[:, :share] + wide(got_qk[:, :share])
    key_raw = kept[:, share : 2 * share] + wide(got_qk[:, share:])
    value_rows = low(kept[:, 2 * share :] + wide(got_v))

    gate_own = take_columns(gate_weight, col * hidden, hidden)
    gate_other = swap(take_columns(gate_weight, (1 - col) * hidden, hidden), "col", 1)
    up_own = take_columns(up_weight, col * hidden, hidden)
    up_other = swap(take_columns(up_weight, (1 - col) * hidden, hidden), "col", 1)
    down_own = take_rows(down_weight, col * hidden, hidden)
    down_other = swap(take_rows(down_weight, (1 - col) * hidden, hidden), "col", 1)
    gate_all = jnp.concatenate([gate_own, gate_other], axis=0)
    up_all = jnp.concatenate([up_own, up_other], axis=0)
    down_all = jnp.concatenate([down_own, down_other], axis=1)

    totals = head_totals(
        jnp.stack([jnp.sum(query_raw * query_raw, axis=1), jnp.sum(key_raw * key_raw, axis=1)])
    )
    query_scale = lax.rsqrt(totals[0] / D + epsilon)[:, None]
    key_scale = lax.rsqrt(totals[1] / D + epsilon)[:, None]
    query_unit = query_raw * query_scale
    key_unit = key_raw * key_scale
    queries = low(rotate_rows(query_unit * query_gain, cosine_table, sine_table))
    key_rows = low(rotate_rows(key_unit * key_gain, cosine_table, sine_table))
    mixed, log_totals = attention_forward(queries, key_rows, value_rows, block_rows)
    gathered_mixed = both_columns(mixed)
    branch = rows_reduced(ordered_block(project(gathered_mixed, output_weight), rows))
    branch_total = pair_total(jnp.sum(branch * branch, axis=1))
    branch_scale = lax.rsqrt(branch_total / D + epsilon)[:, None]
    branch_unit = branch * branch_scale
    hidden_state = wide(layer_in) + branch_unit * mixing_gain

    state_blocks, state_all = all_features(low(hidden_state))
    gate_share = project(state_all, gate_all)
    up_share = project(state_all, up_all)
    activated = low(jax.nn.silu(gate_share) * up_share)
    down_rows = features_reduced(project(activated, down_all), rows)
    gathered_act = both_columns(activated)

    upstream = wide(out_grad)
    down_sums = pair_total(
        jnp.stack(
            [
                jnp.sum(down_rows * down_rows, axis=1),
                jnp.sum(upstream * hidden_gain * down_rows, axis=1),
            ]
        )
    )
    down_scale = lax.rsqrt(down_sums[0] / D + epsilon)[:, None]
    down_unit = down_rows * down_scale
    layer_out = low(hidden_state + down_unit * hidden_gain)
    hidden_part = jnp.sum(upstream * down_unit, axis=0)
    grad_down = norm_backward(upstream, down_rows, down_scale, hidden_gain, down_sums[1])
    gdown_blocks, gdown_all = all_features(low(grad_down))
    gdown_own = jnp.concatenate(gdown_blocks, axis=0)
    down_grad = weight_total(outer_sum(gathered_act, gdown_own), 4, 0)

    grad_act = project_back(gdown_all, down_all)
    gate_sigmoid = jax.nn.sigmoid(gate_share)
    grad_gate = low(grad_act * up_share * (gate_sigmoid * (1.0 + gate_share * (1.0 - gate_sigmoid))))
    grad_up = low(grad_act * jax.nn.silu(gate_share))
    state_own = jnp.concatenate(state_blocks, axis=0)
    gathered_ggate = both_columns(grad_gate)
    gathered_gup = both_columns(grad_up)
    gate_grad = weight_total(outer_sum(state_own, gathered_ggate), 4, 0)
    up_grad = weight_total(outer_sum(state_own, gathered_gup), 4, 0)
    grad_state = upstream + features_reduced(
        project_back(grad_gate, gate_all) + project_back(grad_up, up_all), rows
    )
    mixing_part = jnp.sum(grad_state * branch_unit, axis=0)
    branch_dot = pair_total(jnp.sum(grad_state * mixing_gain * branch, axis=1))
    grad_branch = norm_backward(grad_state, branch, branch_scale, mixing_gain, branch_dot)
    gathered_gbranch = in_order(row_blocks(low(grad_branch)))
    output_grad = weight_total(outer_sum(gathered_mixed, gathered_gbranch), 1, 0)
    other_mixed = project_back(gathered_gbranch, take_rows(output_weight, (1 - col) * share, share))
    own_mixed = project_back(gathered_gbranch, take_rows(output_weight, col * share, share))
    grad_mixed = low(own_mixed + wide(swap(low(other_mixed), "col", 1)))
    grad_queries, grad_keys, grad_values = attention_backward(
        queries, key_rows, value_rows, grad_mixed, log_totals, block_rows
    )
    grad_qnorm = unrotate_rows(grad_queries, cosine_table, sine_table)
    grad_knorm = unrotate_rows(grad_keys, cosine_table, sine_table)
    query_gain_part = jnp.sum(grad_qnorm * query_unit, axis=0)
    key_gain_part = jnp.sum(grad_knorm * key_unit, axis=0)
    dots = head_totals(
        jnp.stack(
            [
                jnp.sum(grad_qnorm * query_gain * query_raw, axis=1),
                jnp.sum(grad_knorm * key_gain * key_raw, axis=1),
            ]
        )
    )
    gathered_gvalue = both_columns(low(grad_values))
    grad_qraw = low(norm_backward(grad_qnorm, query_raw, query_scale, query_gain, dots[0]))
    grad_kraw = low(norm_backward(grad_knorm, key_raw, key_scale, key_gain, dots[1]))
    gathered_gquery = both_columns(grad_qraw)
    gathered_gkey = both_columns(grad_kraw)
    value_grad = weight_total(outer_sum(gathered_in, gathered_gvalue), 1, 0)
    query_grad = weight_total(outer_sum(gathered_in, gathered_gquery), 1, 0)
    key_grad = weight_total(outer_sum(gathered_in, gathered_gkey), 1, 0)
    in_partials = (
        project_back(gathered_gvalue, value_weight)
        + project_back(gathered_gquery, query_weight)
        + project_back(gathered_gkey, key_weight)
    )
    in_grad = low(grad_state + rows_reduced(ordered_block(in_partials, rows)))

    norm_parts = jnp.concatenate([mixing_part, hidden_part])
    for mask in (1, 2):
        norm_parts = norm_parts + swap(norm_parts, "row", mask)
    gain_parts = sequences_summed(
        jnp.concatenate([norm_parts, query_gain_part, key_gain_part])
    )
    wide_count = mixing_part.shape[0]
    narrow_count = query_gain_part.shape[0]
    ends = (wide_count, 2 * wide_count, 2 * wide_count + narrow_count)
    mixing_grad, hidden_grad, query_gain_grad, key_gain_grad = jnp.split(gain_parts, ends)
    return (
        layer_out,
        in_grad,
        query_grad,
        key_grad,
        value_grad,
        output_grad,
        gate_grad,
        up_grad,
        down_grad,
        query_gain_grad,
        key_gain_grad,
        mixing_grad,
        hidden_grad,
    )


def solution(mesh):
    placed = (
        P(("dp", "row"), "col"),
        P("col", "row"),
        P("col", "row"),
        P("col", "row"),
        P("row", "col"),
        P("col", "row"),
        P("col", "row"),
        P("row", "col"),
        P(("row", "col")),
        P(("row", "col")),
        P("col"),
        P("col"),
        P(("dp", "row"), "col"),
    )
    return jax.shard_map(
        local,
        mesh=mesh,
        in_specs=placed,
        out_specs=(
            P(("dp", "row"), "col"),
            P(("dp", "row"), "col"),
            P("col", "row"),
            P("col", "row"),
            P("col", "row"),
            P("row", "col"),
            P("col", "row"),
            P("col", "row"),
            P("row", "col"),
            P(("row", "col")),
            P(("row", "col")),
            P("col"),
            P("col"),
        ),
        check_vma=False,
    )
```

```python
from functools import partial

import jax
import jax.numpy as jnp
from jax import lax
from jax.experimental import pallas as pl
from jax.experimental.pallas import tpu as pltpu
from jax.sharding import PartitionSpec as P

D = 2048
HD = 128
LEN = 1024


epsilon = 1e-06
rope_base = 500000.0
masked_value = -1e30


def low(values):
    return values.astype(jnp.bfloat16)


def wide(values):
    return values.astype(jnp.float32)


def tie(*values):
    return lax.optimization_barrier(values)


def swap(values, axis, mask, name):
    count = lax.axis_size(axis)
    with jax.named_scope(name):
        return lax.ppermute(values, axis, [(i, i ^ mask) for i in range(count)])


def take_rows(values, first, count):
    return lax.dynamic_slice_in_dim(values, first, count, axis=0)


def take_columns(values, first, count):
    return lax.dynamic_slice_in_dim(values, first, count, axis=1)


def row_blocks(shard_rows, name):
    across = swap(shard_rows, "row", 2, name + "_y")
    beside = swap(shard_rows, "row", 1, name + "_c")
    return [shard_rows, beside, across, swap(across, "row", 1, name + "_yc")]


def in_order(blocks):
    row = lax.axis_index("row")
    rows = blocks[0].shape[0]
    result = jnp.concatenate(blocks, axis=0)
    return jnp.concatenate(
        [take_rows(result, (row ^ k) * rows, rows) for k in range(len(blocks))], axis=0
    )


def relative(blocks):
    return jnp.concatenate([blocks[0], blocks[2], blocks[1], blocks[3]], axis=0)


def rows_reduced(partials, name):
    row = lax.axis_index("row")
    rows = partials.shape[0] // 4
    block = lambda k: take_rows(partials, (row ^ k) * rows, rows)
    sent = jnp.concatenate([block(1), block(3)], axis=0)
    got = swap(low(sent), "row", 1, name + "_c")
    other = low(wide(block(2)) + wide(got[rows:]))
    got_other = swap(other, "row", 2, name + "_y")
    return wide(block(0)) + wide(got[:rows]) + wide(got_other)


def features_reduced(kept, sent, name):
    rows = kept.shape[0] // 2
    part = kept.shape[1] // 4
    got = swap(sent, "row", 1, name + "_c")

    def piece(row_slice, first):
        columns = slice(first * part, (first + 1) * part)
        return wide(kept[row_slice, columns]) + wide(got[row_slice, columns])

    mine = slice(0, rows)
    theirs = slice(rows, 2 * rows)
    every = slice(0, 2 * rows)
    a_sent = low(jnp.concatenate([piece(theirs, 0), piece(theirs, 2)], axis=1))
    b_sent = low(piece(every, 3))
    a_got = swap(a_sent, "row", 2, name + "_ay")
    b_got = swap(b_sent, "col", 1, name + "_bx")
    a_other = low(piece(mine, 2) + wide(a_got[:, part:]))
    b_other = low(piece(theirs, 1) + wide(b_got[rows:]))
    a_last = swap(a_other, "col", 1, name + "_ax")
    b_last = swap(b_other, "row", 2, name + "_by")
    a_sum = piece(mine, 0) + wide(a_got[:, :part]) + wide(a_last)
    b_sum = piece(mine, 1) + wide(b_got[:rows]) + wide(b_last)
    return jnp.concatenate([a_sum, b_sum], axis=1)


def both_columns(values, other):
    first = lax.axis_index("col") == 0
    return jnp.concatenate(
        [jnp.where(first, values, other), jnp.where(first, other, values)], axis=1
    )


def all_features(shard_rows, name):
    across = swap(shard_rows, "row", 2, name + "_y")
    other = swap(shard_rows, "col", 1, name + "_x")
    beside = swap(shard_rows, "row", 1, name + "_c")
    own = relative([shard_rows, beside, across, swap(across, "row", 1, name + "_yc")])
    other_across = swap(other, "row", 2, name + "_xy")
    other_beside = swap(other, "row", 1, name + "_xc")
    pair = relative(
        [other, other_beside, other_across, swap(other_across, "row", 1, name + "_xyc")]
    )
    return own, pair


def pair_total(sums, name):
    return sums + swap(sums, "col", 1, name)


def head_totals(sums, name):
    for axis, mask in (("row", 1), ("row", 2), ("col", 1)):
        sums = sums + swap(sums, axis, mask, name + axis + str(mask))
    return sums


def place_kernel(where_ref, flag_ref, *refs):
    total_ref, outward_ref, out_ref = refs[-3:]
    inner = flag_ref[0] == 1
    out_ref[...] = jnp.where(inner, total_ref[...], outward_ref[...]).astype(jnp.float32)


def place(result, shape, total, outward, row_block, column_block, inner):
    rows, columns = total.shape
    step = rows if rows < 256 else 256
    count = rows // step
    at = jnp.stack([row_block * count, column_block]).astype(jnp.int32)
    flag = jnp.reshape(inner, (1,)).astype(jnp.int32)
    piece_spec = pl.BlockSpec((step, columns), lambda i, at, flag: (i, 0))
    out_spec = pl.BlockSpec((step, columns), lambda i, at, flag: (at[0] + i, at[1]))
    held = [] if result is None else [result]
    return pl.pallas_call(
        place_kernel,
        out_shape=jax.ShapeDtypeStruct(shape, jnp.float32),
        grid_spec=pltpu.PrefetchScalarGridSpec(
            num_scalar_prefetch=2,
            grid=(count,),
            in_specs=[pl.BlockSpec(memory_space=pl.ANY)] * len(held) + [piece_spec, piece_spec],
            out_specs=out_spec,
        ),
        input_output_aliases={2: 0} if held else {},
    )(at, flag, *held, total, outward)


class Stream:
    def __init__(self, depth):
        self.depth = depth
        self.stages = ([], [], [])
        self.results = {}
        self.at = lax.axis_index("dp")
        self.line = lax.axis_size("dp") == 4
        self.inner = (self.at == 1) | (self.at == 2)
        self.count = 0

    def send(self, values, stage):
        pairs = ([(0, 1), (3, 2)], [(1, 2), (2, 1)], [(1, 0), (2, 3)])[stage]
        with jax.named_scope("z%d_%d" % (stage, self.count)):
            return lax.ppermute(values, "dp", pairs)

    def put(self, key, total, outward):
        name, shape, row_block, column_block = key
        self.results[name] = place(
            self.results.get(name), shape, total, outward, row_block, column_block, self.inner
        )

    def step(self, new, *carry):
        self.count += 1
        if not self.line:
            if new is not None:
                key, piece = new
                total = lax.psum(piece, "dp")
                self.put(key, total, total)
            return carry
        ready = []
        for stage in self.stages:
            full = len(stage) >= self.depth or (new is None and stage)
            ready.append(stage.pop(0) if full else None)
        arrived = [item[2] for item in ready if item is not None]
        if new is not None:
            arrived.append(new[1])
        tied = tie(*arrived, *carry)
        carry = tied[len(arrived) :]
        tied = list(tied[: len(arrived)])
        ready = [None if item is None else (item[0], item[1], tied.pop(0)) for item in ready]
        if ready[0] is not None:
            key, own, got = ready[0]
            half = low(wide(own) + wide(got))
            self.stages[1].append((key, half, self.send(half, 1)))
        if ready[1] is not None:
            key, own, got = ready[1]
            total = low(wide(own) + wide(got))
            self.stages[2].append((key, total, self.send(total, 2)))
        if new is not None:
            piece = tied.pop(0)
            self.stages[0].append((new[0], piece, self.send(piece, 0)))
        if ready[2] is not None:
            self.put(*ready[2])
        return carry

    def busy(self):
        return any(self.stages)


def sequences_summed(partials):
    if lax.axis_size("dp") != 4:
        return lax.psum(partials, "dp")
    at = lax.axis_index("dp")
    inner = (at == 1) | (at == 2)
    with jax.named_scope("gains"):
        half = partials + lax.ppermute(partials, "dp", [(0, 1), (3, 2)])
        total = half + lax.ppermute(half, "dp", [(1, 2), (2, 1)])
        outward = lax.ppermute(total, "dp", [(1, 0), (2, 3)])
    return jnp.where(inner, total, outward)


def project(left_rows, right_rows):
    return jnp.dot(left_rows, right_rows, preferred_element_type=jnp.float32)


def project_back(left_rows, right_rows):
    return lax.dot_general(
        left_rows, right_rows, (((1,), (1,)), ((), ())), preferred_element_type=jnp.float32
    )


def outer_sum(left_rows, right_rows):
    return lax.dot_general(
        left_rows, right_rows, (((0,), (0,)), ((), ())), preferred_element_type=jnp.float32
    )


def rotary_tables(row_count):
    positions = (jnp.arange(row_count, dtype=jnp.int32) % LEN).astype(jnp.float32)
    exponent = jnp.arange(HD // 2, dtype=jnp.float32) * (2.0 / HD)
    freq_rows = rope_base ** (-exponent)
    angles = positions[:, None] * freq_rows[None, :]
    angles = jnp.concatenate([angles, angles], axis=1)
    return (jnp.cos(angles), jnp.sin(angles))


def turn_half(values):
    first_half = values[..., : HD // 2]
    second_half = values[..., HD // 2 :]
    return jnp.concatenate([-second_half, first_half], axis=-1)


def turn_back(values):
    first_half = values[..., : HD // 2]
    second_half = values[..., HD // 2 :]
    return jnp.concatenate([second_half, -first_half], axis=-1)


def rotate_rows(row_values, cosine_table, sine_table):
    shaped = row_values.reshape(row_values.shape[0], -1, HD)
    turned = shaped * cosine_table[:, None, :] + turn_half(shaped) * sine_table[:, None, :]
    return turned.reshape(row_values.shape[0], -1)


def unrotate_rows(row_values, cosine_table, sine_table):
    shaped = row_values.reshape(row_values.shape[0], -1, HD)
    turned = shaped * cosine_table[:, None, :] + turn_back(shaped * sine_table[:, None, :])
    return turned.reshape(row_values.shape[0], -1)


def norm_backward(upstream, raw_rows, row_scale, gain_slice, dot_total):
    scaled = upstream * gain_slice
    return (
        row_scale * scaled
        - raw_rows * (row_scale * row_scale * row_scale) * (dot_total / D)[:, None]
    )


def masked_scores(query_block, key_four, first_row, block_rows):
    raw_scores = jnp.einsum(
        "sqhe,skhe->shqk", query_block, key_four, preferred_element_type=jnp.float32
    ) * HD ** (-0.5)
    query_index = first_row + jnp.arange(block_rows, dtype=jnp.int32)
    causal = query_index[:, None] >= jnp.arange(LEN, dtype=jnp.int32)[None, :]
    return jnp.where(causal, raw_scores, masked_value)


def attention_forward(queries, key_rows, value_rows, block_rows):
    group_rows = queries.shape[0]
    seq_count = group_rows // LEN
    query_four = queries.reshape(seq_count, LEN, -1, HD)
    key_four = key_rows.reshape(seq_count, LEN, -1, HD)
    value_four = value_rows.reshape(seq_count, LEN, -1, HD)
    outputs = []
    log_parts = []
    for block_index in range(LEN // block_rows):
        first_row = block_index * block_rows
        query_block = query_four[:, first_row : first_row + block_rows]
        scores = masked_scores(query_block, key_four, first_row, block_rows)
        row_peak = jnp.max(scores, axis=-1, keepdims=True)
        spread = jnp.exp(scores - row_peak)
        row_total = jnp.sum(spread, axis=-1, keepdims=True)
        soft_weights = (spread / row_total).astype(jnp.bfloat16)
        outputs.append(
            jnp.einsum(
                "shqk,skhe->sqhe", soft_weights, value_four, preferred_element_type=jnp.float32
            )
        )
        log_parts.append((row_peak + jnp.log(row_total))[..., 0])
    mixed = jnp.concatenate(outputs, axis=1).reshape(group_rows, -1).astype(jnp.bfloat16)
    return (mixed, jnp.concatenate(log_parts, axis=2))


def attention_backward(queries, key_rows, value_rows, grad_mixed, log_totals, block_rows):
    group_rows = queries.shape[0]
    seq_count = group_rows // LEN
    query_four = queries.reshape(seq_count, LEN, -1, HD)
    key_four = key_rows.reshape(seq_count, LEN, -1, HD)
    value_four = value_rows.reshape(seq_count, LEN, -1, HD)
    grad_four = grad_mixed.reshape(seq_count, LEN, -1, HD)
    score_scale = HD ** (-0.5)
    grad_keys = jnp.zeros(key_four.shape, jnp.float32)
    grad_values = jnp.zeros(value_four.shape, jnp.float32)
    query_parts = []
    for block_index in range(LEN // block_rows):
        first_row = block_index * block_rows
        query_block = query_four[:, first_row : first_row + block_rows]
        grad_block = grad_four[:, first_row : first_row + block_rows]
        scores = masked_scores(query_block, key_four, first_row, block_rows)
        soft_float = jnp.exp(scores - log_totals[:, :, first_row : first_row + block_rows, None])
        soft_weights = soft_float.astype(jnp.bfloat16)
        grad_values = grad_values + jnp.einsum(
            "shqk,sqhe->skhe", soft_weights, grad_block, preferred_element_type=jnp.float32
        )
        grad_soft = jnp.einsum(
            "sqhe,skhe->shqk", grad_block, value_four, preferred_element_type=jnp.float32
        )
        centre = jnp.sum(soft_float * grad_soft, axis=-1, keepdims=True)
        grad_scores = (soft_float * (grad_soft - centre)).astype(jnp.bfloat16)
        query_parts.append(
            jnp.einsum("shqk,skhe->sqhe", grad_scores, key_four, preferred_element_type=jnp.float32)
            * score_scale
        )
        grad_keys = (
            grad_keys
            + jnp.einsum(
                "shqk,sqhe->skhe", grad_scores, query_block, preferred_element_type=jnp.float32
            )
            * score_scale
        )
    grad_queries = jnp.concatenate(query_parts, axis=1).reshape(group_rows, -1)
    return (grad_queries, grad_keys.reshape(group_rows, -1), grad_values.reshape(group_rows, -1))


def local(
    layer_in,
    query_weight,
    key_weight,
    value_weight,
    output_weight,
    gate_weight,
    up_weight,
    down_weight,
    query_gain,
    key_gain,
    mixing_gain,
    hidden_gain,
    out_grad,
):
    rows = layer_in.shape[0]
    tokens = rows * lax.axis_size("row")
    half_tokens = tokens // 2
    block_rows = min(512, LEN)
    col = lax.axis_index("col")
    parity = lax.axis_index("dp") % 2
    cosine_table, sine_table = rotary_tables(tokens)

    share = query_weight.shape[1] // 2
    hidden = gate_weight.shape[1] // 2
    width = layer_in.shape[1]
    part = width // 2
    own_projection = jnp.concatenate(
        [take_columns(w, col * share, share) for w in (query_weight, key_weight, value_weight)], axis=1
    )
    other_projection = [
        take_columns(w, (1 - col) * share, share) for w in (query_weight, key_weight, value_weight)
    ]
    other_qk = jnp.concatenate(other_projection[:2], axis=1)
    other_v = other_projection[2]

    gate_sent = lax.dynamic_slice(gate_weight, (parity * part, (1 - col) * hidden), (part, hidden))
    up_sent = lax.dynamic_slice(up_weight, (parity * part, (1 - col) * hidden), (part, hidden))
    unit_part = hidden // 2
    down_sent = take_rows(down_weight, (1 - col) * hidden + parity * unit_part, unit_part)

    def halves(fetched, traded):
        return jnp.where(parity == 0, fetched, traded), jnp.where(parity == 0, traded, fetched)

    in_blocks = row_blocks(layer_in, "in")
    gate_x = swap(gate_sent, "col", 1, "gate_x")
    gathered_in = in_order(in_blocks)

    sent_qk = low(project(gathered_in, other_qk))
    got_qk = swap(sent_qk, "col", 1, "qk_x")
    sent_v = low(project(gathered_in, other_v))
    got_v = swap(sent_v, "col", 1, "v_x")
    kept = project(gathered_in, own_projection)
    got_qk, gate_x, kept = tie(got_qk, gate_x, kept)
    gate_z = swap(gate_x, "dp", 1, "gate_z")
    query_raw = kept[:, :share] + wide(got_qk[:, :share])
    key_raw = kept[:, share : 2 * share] + wide(got_qk[:, share:])
    totals = head_totals(
        jnp.stack([jnp.sum(query_raw * query_raw, axis=1), jnp.sum(key_raw * key_raw, axis=1)]),
        "qk_sums",
    )
    totals, got_v, up_sent = tie(totals, got_v, up_sent)
    up_x = swap(up_sent, "col", 1, "up_x")
    value_rows = low(kept[:, 2 * share :] + wide(got_v))
    query_scale = lax.rsqrt(totals[0] / D + epsilon)[:, None]
    key_scale = lax.rsqrt(totals[1] / D + epsilon)[:, None]
    query_unit = query_raw * query_scale
    key_unit = key_raw * key_scale
    queries = low(rotate_rows(query_unit * query_gain, cosine_table, sine_table))
    key_rows = low(rotate_rows(key_unit * key_gain, cosine_table, sine_table))
    mixed, log_totals = attention_forward(queries, key_rows, value_rows, block_rows)
    mixed, up_x, gate_z = tie(mixed, up_x, gate_z)
    mixed_other = swap(mixed, "col", 1, "mixed_x")
    up_z = swap(up_x, "dp", 1, "up_z")
    gate_own = take_columns(gate_weight, col * hidden, hidden)
    gate_all = jnp.concatenate([gate_own, *halves(gate_x, gate_z)], axis=0)
    mixed_other, down_sent, gate_all = tie(mixed_other, down_sent, gate_all)
    down_x = swap(down_sent, "col", 1, "down_x")
    gathered_mixed = both_columns(mixed, mixed_other)
    branch = rows_reduced(low(project(gathered_mixed, output_weight)), "branch")
    branch, up_z = tie(branch, up_z)
    up_own = take_columns(up_weight, col * hidden, hidden)
    up_all = jnp.concatenate([up_own, *halves(up_x, up_z)], axis=0)
    branch_total = pair_total(jnp.sum(branch * branch, axis=1), "branch_sum")
    branch_total, up_all, down_x = tie(branch_total, up_all, down_x)
    down_z = swap(down_x, "dp", 1, "down_z")
    branch_scale = lax.rsqrt(branch_total / D + epsilon)[:, None]
    branch_unit = branch * branch_scale
    hidden_state = wide(layer_in) + branch_unit * mixing_gain

    state_own, state_other = all_features(low(hidden_state), "state")
    state_own, state_other, down_z = tie(state_own, state_other, down_z)
    state_all = jnp.concatenate([state_own, state_other], axis=1)
    down_own = take_rows(down_weight, col * hidden, hidden)
    down_all = jnp.concatenate(
        [down_own, jnp.concatenate(halves(down_x, down_z), axis=0)], axis=1
    )
    gate_share = project(state_all, gate_all)
    up_share = project(state_all, up_all)
    activated = low(jax.nn.silu(gate_share) * up_share)
    down_sent_rows = low(project(activated[half_tokens:], down_all))
    down_kept_rows = low(project(activated[:half_tokens], down_all))
    down_rows = features_reduced(down_kept_rows, down_sent_rows, "down")

    upstream = wide(out_grad)
    down_sums = pair_total(
        jnp.stack(
            [
                jnp.sum(down_rows * down_rows, axis=1),
                jnp.sum(upstream * hidden_gain * down_rows, axis=1),
            ]
        ),
        "down_sums",
    )
    down_scale = lax.rsqrt(down_sums[0] / D + epsilon)[:, None]
    down_unit = down_rows * down_scale
    layer_out = low(hidden_state + down_unit * hidden_gain)
    hidden_part = jnp.sum(upstream * down_unit, axis=0)
    grad_down = low(norm_backward(upstream, down_rows, down_scale, hidden_gain, down_sums[1]))
    act_parts = [activated[:, :unit_part], activated[:, unit_part:]]
    gdown_own, gdown_other = all_features(grad_down, "gdown")

    gate_shape = gate_weight.shape
    down_shape = down_weight.shape
    small_shape = query_weight.shape
    stream = Stream(1)

    def down_piece(source, which, index):
        return ("down", down_shape, which * 2 + index, 0), low(
            outer_sum(source[:, index * unit_part : (index + 1) * unit_part], gdown_own)
        )

    def unit_piece(name, source, which, index):
        return (name, gate_shape, index, which), low(
            outer_sum(state_own[:, index * part : (index + 1) * part], source)
        )

    (gdown_own,) = stream.step(down_piece(activated, col, 0), gdown_own)
    act_x = [swap(act, "col", 1, "act_x%d" % i) for i, act in enumerate(act_parts)]
    gdown_all = jnp.concatenate([gdown_own, gdown_other], axis=1)
    grad_act = project_back(gdown_all, down_all)
    gate_sigmoid = jax.nn.sigmoid(gate_share)
    grad_gate = low(grad_act * up_share * (gate_sigmoid * (1.0 + gate_share * (1.0 - gate_sigmoid))))
    grad_up = low(grad_act * jax.nn.silu(gate_share))
    grad_gate, grad_up = stream.step(down_piece(activated, col, 1), grad_gate, grad_up)
    state_sent_rows = low(
        project_back(grad_gate[half_tokens:], gate_all) + project_back(grad_up[half_tokens:], up_all)
    )
    state_kept_rows = low(
        project_back(grad_gate[:half_tokens], gate_all) + project_back(grad_up[:half_tokens], up_all)
    )
    act_other = jnp.concatenate(act_x, axis=1)
    state_sent_rows, state_kept_rows, act_other = stream.step(
        unit_piece("gate", grad_gate, col, 0), state_sent_rows, state_kept_rows, act_other
    )
    grad_state = upstream + features_reduced(state_kept_rows, state_sent_rows, "gstate")
    grad_state, grad_gate, grad_up = stream.step(
        unit_piece("gate", grad_gate, col, 1), grad_state, grad_gate, grad_up
    )
    gate_halves = [grad_gate[:, :unit_part], grad_gate[:, unit_part:]]
    up_halves = [grad_up[:, :unit_part], grad_up[:, unit_part:]]
    mixing_part = jnp.sum(grad_state * branch_unit, axis=0)
    branch_dot = pair_total(jnp.sum(grad_state * mixing_gain * branch, axis=1), "branch_dot")
    grad_branch = low(norm_backward(grad_state, branch, branch_scale, mixing_gain, branch_dot))
    gbranch_blocks = row_blocks(grad_branch, "gbranch")
    gbranch_blocks = stream.step(
        down_piece(act_other, 1 - col, 0), *gbranch_blocks
    )
    gathered_gbranch = in_order(gbranch_blocks)
    other_mixed = low(
        project_back(gathered_gbranch, take_rows(output_weight, (1 - col) * share, share))
    )
    gmixed_x = swap(other_mixed, "col", 1, "gmixed_x")
    own_mixed = project_back(gathered_gbranch, take_rows(output_weight, col * share, share))
    gmixed_x, own_mixed, *gate_halves = stream.step(
        down_piece(act_other, 1 - col, 1), gmixed_x, own_mixed, *gate_halves
    )
    ggate_x = [swap(part_of, "col", 1, "ggate_x%d" % i) for i, part_of in enumerate(gate_halves)]
    grad_mixed = low(own_mixed + wide(gmixed_x))
    grad_queries, grad_keys, grad_values = attention_backward(
        queries, key_rows, value_rows, grad_mixed, log_totals, block_rows
    )
    grad_queries, grad_keys, grad_values, ggate_x[0] = stream.step(
        unit_piece("up", grad_up, col, 0), grad_queries, grad_keys, grad_values, ggate_x[0]
    )
    grad_qnorm = unrotate_rows(grad_queries, cosine_table, sine_table)
    grad_knorm = unrotate_rows(grad_keys, cosine_table, sine_table)
    query_gain_part = jnp.sum(grad_qnorm * query_unit, axis=0)
    key_gain_part = jnp.sum(grad_knorm * key_unit, axis=0)
    dots = head_totals(
        jnp.stack(
            [
                jnp.sum(grad_qnorm * query_gain * query_raw, axis=1),
                jnp.sum(grad_knorm * key_gain * key_raw, axis=1),
            ]
        ),
        "qk_dots",
    )
    dots, ggate_x[1], grad_values, *up_halves = stream.step(
        unit_piece("up", grad_up, col, 1), dots, ggate_x[1], grad_values, *up_halves
    )
    ggate_other = jnp.concatenate(ggate_x, axis=1)
    gup_x = [swap(up_halves[0], "col", 1, "gup_x0")]
    grad_qraw = low(norm_backward(grad_qnorm, query_raw, query_scale, query_gain, dots[0]))
    grad_kraw = low(norm_backward(grad_knorm, key_raw, key_scale, key_gain, dots[1]))
    gup_x[0], grad_qraw, grad_kraw, grad_vraw = stream.step(
        unit_piece("gate", ggate_other, 1 - col, 0), gup_x[0], grad_qraw, grad_kraw, low(grad_values)
    )
    gup_x.append(swap(up_halves[1], "col", 1, "gup_x1"))
    gup_x[1], grad_qraw, grad_kraw, grad_vraw = stream.step(
        unit_piece("gate", ggate_other, 1 - col, 1), gup_x[1], grad_qraw, grad_kraw, grad_vraw
    )
    gup_other = jnp.concatenate(gup_x, axis=1)
    gvalue_x = swap(grad_vraw, "col", 1, "gv_x")
    gquery_x = swap(grad_qraw, "col", 1, "gq_x")
    gvalue_x, gquery_x, grad_kraw = stream.step(
        unit_piece("up", gup_other, 1 - col, 0), gvalue_x, gquery_x, grad_kraw
    )
    gkey_x = swap(grad_kraw, "col", 1, "gk_x")
    gathered_gvalue = both_columns(grad_vraw, gvalue_x)
    gathered_gquery = both_columns(grad_qraw, gquery_x)
    gkey_x, gathered_gvalue, gathered_gquery = stream.step(
        unit_piece("up", gup_other, 1 - col, 1), gkey_x, gathered_gvalue, gathered_gquery
    )
    gathered_gkey = both_columns(grad_kraw, gkey_x)
    in_partials = low(
        project_back(gathered_gvalue, value_weight)
        + project_back(gathered_gquery, query_weight)
        + project_back(gathered_gkey, key_weight)
    )
    (in_partials,) = stream.step(
        (("output", output_weight.shape, 0, 0), low(outer_sum(gathered_mixed, gathered_gbranch))),
        in_partials,
    )
    in_grad = low(grad_state + rows_reduced(in_partials, "gin"))
    norm_parts = jnp.concatenate([mixing_part, hidden_part])
    for mask in (1, 2):
        norm_parts = norm_parts + swap(norm_parts, "row", mask, "norm_parts%d" % mask)
    in_grad, norm_parts = stream.step(
        (("value", small_shape, 0, 0), low(outer_sum(gathered_in, gathered_gvalue))),
        in_grad,
        norm_parts,
    )
    gain_parts = sequences_summed(jnp.concatenate([norm_parts, query_gain_part, key_gain_part]))
    stream.step((("query", small_shape, 0, 0), low(outer_sum(gathered_in, gathered_gquery))))
    (gain_parts,) = stream.step(
        (("key", small_shape, 0, 0), low(outer_sum(gathered_in, gathered_gkey))), gain_parts
    )
    while stream.busy():
        stream.step(None)

    wide_count = mixing_part.shape[0]
    narrow_count = query_gain_part.shape[0]
    ends = (wide_count, 2 * wide_count, 2 * wide_count + narrow_count)
    mixing_grad, hidden_grad, query_gain_grad, key_gain_grad = jnp.split(gain_parts, ends)
    return (
        layer_out,
        in_grad,
        stream.results["query"],
        stream.results["key"],
        stream.results["value"],
        stream.results["output"],
        stream.results["gate"],
        stream.results["up"],
        stream.results["down"],
        query_gain_grad,
        key_gain_grad,
        mixing_grad,
        hidden_grad,
    )


def solution(mesh):
    placed = (
        P(("dp", "row"), "col"),
        P("col", "row"),
        P("col", "row"),
        P("col", "row"),
        P("row", "col"),
        P("col", "row"),
        P("col", "row"),
        P("row", "col"),
        P(("row", "col")),
        P(("row", "col")),
        P("col"),
        P("col"),
        P(("dp", "row"), "col"),
    )
    return jax.shard_map(
        local,
        mesh=mesh,
        in_specs=placed,
        out_specs=(
            P(("dp", "row"), "col"),
            P(("dp", "row"), "col"),
            P("col", "row"),
            P("col", "row"),
            P("col", "row"),
            P("row", "col"),
            P("col", "row"),
            P("col", "row"),
            P("row", "col"),
            P(("row", "col")),
            P(("row", "col")),
            P("col"),
            P("col"),
        ),
        check_vma=False,
    )
```
